32 devices in a mesh: seq: 8 (over y, x, core), head: 4 (over z).
Axes of the slice: x: 2, y: 2, z: 4, core: 2. Of those that a mesh axis runs over, the one named last changes fastest.
Arguments:
- inputs: bfloat16 [4096, 4096], P('seq'), may hold values from -6 to 6
- queries: bfloat16 [4096, 4096], P('seq', 'head'), may hold values from -6 to 6
- keys: bfloat16 [4096, 4096], P('seq', 'head'), may hold values from -6 to 6
- values: bfloat16 [4096, 4096], P('seq', 'head'), may hold values from -6 to 6
- out_grad: bfloat16 [4096, 4096], P('seq', 'head'), may hold values from -6 to 6
- value_weight: bfloat16 [4096, 4096], P('seq', 'head'), may hold values from -0.125 to 0.125
Outputs:
- grad_input: bfloat16 [4096, 4096], P('seq', 'head')
- grad_query: bfloat16 [4096, 4096], P('seq', 'head')
- grad_key: bfloat16 [4096, 4096], P('seq', 'head')
- grad_value: bfloat16 [4096, 4096], P('seq', 'head')
- grad_weight: float32 [4096, 4096], P('seq', 'head')
The draws below stay inside these ranges and needn't reach their ends.
All inputs are finite; a program needn't handle non-finite values.
Results may differ from the reference program's by a relative error of at most 0.015.
Values may be sent and summed in bfloat16 or wider, within the bound.
A program may use at most 128 MiB of HBM per device.

```python
import jax
import jax.numpy as jnp
from jax import lax

D = 4096
HEADS = 32
HEAD_DIM = 128
TOK_DEV = 512
WIDTH = 4096
BLOCKS = 8
TOKENS = 4096


def with_spikes(drawn, own_key, source, target, parts, factor):
    owner, partner = [(jnp.arange(drawn.shape[dim]) // (drawn.shape[dim] // parts)).reshape([-1 if axis == dim else 1 for axis in range(drawn.ndim)]) for dim in (source, target)]
    chosen = jax.random.permutation(own_key, parts)[partner]
    strong = (owner == chosen) | (owner == (partner + parts // 2) % parts)
    return jnp.where(strong, factor * drawn, drawn)


def level_of(stream_key, extent, shards, smallest, high):
    factor_of, own = 1.0, jax.random.fold_in(stream_key, 6)
    for axis_at, parts in shards:
        steps = jnp.exp(jax.random.uniform(jax.random.fold_in(own, axis_at), (parts,), jnp.float32, smallest / len(shards), high / len(shards)))
        factor_of = factor_of * jnp.repeat(steps, extent[axis_at] // parts).reshape([-1 if axis == axis_at else 1 for axis in range(len(extent))])
    return factor_of


def centred(key, dims, scale, most, cuts=(), kind=jnp.bfloat16):
    result = jax.random.normal(key, dims, jnp.float32) * scale
    if len(cuts) > 0:
        result = level_of(key, dims, cuts, -0.22, 0.18) * result
    return jnp.clip(result, min=-most, max=most).astype(kind)


def heavy_noise(stream_key, extent, width, most, cuts, heavy, held_as=jnp.bfloat16):
    array = width * jax.random.normal(stream_key, extent, jnp.float32)
    if cuts:
        array = array * level_of(stream_key, extent, cuts, -0.22, 0.18)
    return jnp.clip(with_spikes(array, jax.random.fold_in(stream_key, 3), *heavy), -most, most).astype(held_as)


def setup_inputs(seed: int = 0) -> dict:
    key_of = jax.random.split(jax.random.key(seed), 7)
    inputs = heavy_noise(key_of[0], (TOKENS, D), 1.0, 6.0, ((0, 8),), (0, 1, 8, 2.0))
    queries = centred(key_of[1], (TOKENS, WIDTH), 1.0, 6.0, ((0, 8), (1, 4)))
    keys = centred(key_of[2], (TOKENS, WIDTH), 1.0, 6.0, ((0, 8), (1, 4)))
    values = centred(key_of[3], (TOKENS, WIDTH), 1.0, 6.0, ((0, 8), (1, 4)))
    out_grad = centred(key_of[4], (TOKENS, WIDTH), 1.0, 6.0, ((0, 8), (1, 4)))
    value_weight = heavy_noise(key_of[5], (D, WIDTH), D ** -0.5, 0.125, ((0, 8), (1, 4)), (1, 0, 8, 2.0))
    return {"inputs": inputs, "queries": queries, "keys": keys, "values": values, "out_grad": out_grad, "value_weight": value_weight}


def round_trip(a):
    return lax.optimization_barrier(a.astype(jnp.bfloat16)).astype(jnp.float32)

def reference(inputs, queries, keys, values, out_grad, value_weight):
    f32 = jnp.float32
    high = lax.Precision.HIGHEST
    posit = jnp.arange(TOKENS, dtype=jnp.int32).astype(f32)
    factor = 1.0 / jnp.sqrt(HEAD_DIM * (posit + 1.0))

    def split(a):
        return a.astype(f32).reshape(BLOCKS, TOK_DEV, HEADS, HEAD_DIM)
    q4, k4, v4, o4 = (split(queries), split(keys), split(values), split(out_grad))
    fac = factor.reshape(BLOCKS, TOK_DEV)
    state_kv = jnp.einsum('bthi,bthj->bhij', k4, v4, precision=high)
    state_qo = jnp.einsum('bthi,bthj->bhij', q4, o4 * fac[:, :, None, None], precision=high)
    zeros = jnp.zeros_like(state_kv[:1])
    prefix = jnp.concatenate([zeros, jnp.cumsum(state_kv, axis=0)[:-1]], axis=0)
    suffix = jnp.concatenate([jnp.cumsum(state_qo[::-1], axis=0)[:-1][::-1], zeros], axis=0)
    idx = jnp.arange(TOK_DEV, dtype=jnp.int32)
    lower = idx[:, None] >= idx[None, :]

    def block(items):
        qb, kb, vb, ob, cb, pb, sb = items
        sqk = jnp.einsum('thd,shd->hts', qb, kb, precision=high) * cb[None, :, None]
        sqk = round_trip(jnp.where(lower[None], sqk, 0.0))
        sov = jnp.einsum('thd,shd->hts', ob, vb, precision=high) * cb[None, :, None]
        sov = round_trip(jnp.where(lower[None], sov, 0.0))
        dq = jnp.einsum('hts,shd->thd', sov, kb, precision=high) + cb[:, None, None] * jnp.einsum('thj,hij->thi', ob, pb, precision=high)
        dk = jnp.einsum('hts,thd->shd', sov, qb, precision=high) + jnp.einsum('shj,hij->shi', vb, sb, precision=high)
        dv = jnp.einsum('hts,thd->shd', sqk, ob, precision=high) + jnp.einsum('shi,hij->shj', kb, sb, precision=high)
        return (dq.astype(jnp.bfloat16), dk.astype(jnp.bfloat16), dv.astype(jnp.bfloat16))
    dq, dk, dv = lax.map(block, (q4, k4, v4, o4, fac, prefix, suffix))
    grad_query = dq.reshape(TOKENS, WIDTH)
    grad_key = dk.reshape(TOKENS, WIDTH)
    grad_value = dv.reshape(TOKENS, WIDTH)
    grad_input = jnp.dot(grad_value.astype(f32), value_weight.astype(f32).T, precision=high).astype(jnp.bfloat16)
    wscale = TOKENS ** (-0.5)
    xb = inputs.reshape(BLOCKS, TOK_DEV, D)
    gb = grad_value.reshape(BLOCKS, TOK_DEV, WIDTH)

    def accumulate(total, pair):
        term = jnp.dot(pair[0].astype(f32).T, pair[1].astype(f32), precision=high) * wscale
        return (total + round_trip(term), None)
    grad_weight, unused = lax.scan(accumulate, jnp.zeros((D, WIDTH), f32), (xb, gb))
    return (grad_input, grad_query, grad_key, grad_value, grad_weight)
```

```python
import math

import jax
import jax.numpy as jnp
from jax import lax
from jax.sharding import PartitionSpec as P

HEAD_DIM = 128


def exchange(x, axis, bit):
    return lax.ppermute(x, axis, [(i, i ^ bit) for i in range(lax.axis_size(axis))])


def bits_of(axis):
    count = lax.axis_size(axis)
    assert count & (count - 1) == 0
    return [1 << k for k in range(count.bit_length() - 1)]


def carried_in(state, axis, later):
    here = lax.axis_index(axis)
    carried, total = jnp.zeros_like(state), state
    for bit in bits_of(axis):
        got = exchange(total.astype(jnp.bfloat16), axis, bit).astype(state.dtype)
        upper = (here & bit) != 0
        carried = carried + jnp.where(upper != later, got, 0.0)
        total = total + got
    return carried


def halving(terms, axis, bits):
    terms = dict(terms)
    for at, bit in enumerate(bits):
        leaving = [m for m in terms if m & bit]
        ahead = sum(bits[at + 1 :])
        for m in sorted(leaving, key=lambda m: -bin(m & ahead).count("1")):
            got = exchange(terms.pop(m).astype(jnp.bfloat16), axis, bit)
            terms[m ^ bit] = terms[m ^ bit].astype(jnp.float32) + got.astype(jnp.float32)
    return terms[0]


def local(inputs, queries, keys, values, out_grad, value_weight):
    f32 = jnp.float32
    high = lax.Precision.HIGHEST
    rows = queries.shape[0]
    width = queries.shape[1]
    nheads = width // HEAD_DIM
    first = lax.axis_index("seq") * rows
    posit = (first + jnp.arange(rows, dtype=jnp.int32)).astype(f32)
    factor = 1.0 / jnp.sqrt(HEAD_DIM * (posit + 1.0))
    q3 = queries.reshape(rows, nheads, HEAD_DIM)
    k3 = keys.reshape(rows, nheads, HEAD_DIM)
    v3 = values.reshape(rows, nheads, HEAD_DIM)
    o3 = out_grad.reshape(rows, nheads, HEAD_DIM)
    o3wide = o3.astype(f32)
    state_kv = jnp.einsum("thi,thj->hij", k3, v3, preferred_element_type=f32)
    state_qo = jnp.einsum(
        "thi,thj->hij", q3.astype(f32), o3wide * factor[:, None, None], precision=high
    )
    suffix = carried_in(state_qo, "seq", True)
    prefix = carried_in(state_kv, "seq", False)
    index = jnp.arange(rows, dtype=jnp.int32)
    lower = (index[:, None] >= index[None, :])[None]
    score_qk = (
        jnp.einsum("thd,shd->hts", q3, k3, preferred_element_type=f32) * factor[None, :, None]
    )
    score_qk = jnp.where(lower, score_qk, 0.0).astype(jnp.bfloat16)
    score_ov = (
        jnp.einsum("thd,shd->hts", o3, v3, preferred_element_type=f32) * factor[None, :, None]
    )
    score_ov = jnp.where(lower, score_ov, 0.0).astype(jnp.bfloat16)
    dq = jnp.einsum("hts,shd->thd", score_ov, k3, preferred_element_type=f32)
    dq = dq + factor[:, None, None] * jnp.einsum("thj,hij->thi", o3wide, prefix, precision=high)
    dk = jnp.einsum("hts,thd->shd", score_ov, q3, preferred_element_type=f32)
    dk = dk + jnp.einsum("shj,hij->shi", v3.astype(f32), suffix, precision=high)
    dv = jnp.einsum("hts,thd->shd", score_qk, o3, preferred_element_type=f32)
    dv = dv + jnp.einsum("shi,hij->shj", k3.astype(f32), suffix, precision=high)
    grad_query = dq.reshape(rows, width).astype(jnp.bfloat16)
    grad_key = dk.reshape(rows, width).astype(jnp.bfloat16)
    grad_value = dv.reshape(rows, width).astype(jnp.bfloat16)
    here, group = (lax.axis_index("seq"), lax.axis_index("head"))
    weight = lax.all_gather(value_weight, "seq", axis=0, tiled=True)
    span = weight.shape[0] // lax.axis_size("head")
    pieces = {}
    for m in range(lax.axis_size("head")):
        part = lax.dynamic_slice_in_dim(weight, (group ^ m) * span, span, 0)
        pieces[m] = lax.dot_general(
            grad_value, part, (((1,), (1,)), ((), ())), preferred_element_type=f32
        ).astype(jnp.bfloat16)
    grad_input = halving(pieces, "head", bits_of("head")).astype(jnp.bfloat16)
    wscale = 1.0 / math.sqrt(rows * lax.axis_size("seq"))
    slab = inputs.shape[1] // lax.axis_size("seq")
    first_bit, *rest = bits_of("seq")
    masks = [m for m in range(lax.axis_size("seq"))]
    sides = []
    for side in (first_bit, 0):
        chosen = [m for m in masks if m & first_bit == side]
        picked = jnp.concatenate(
            [lax.dynamic_slice_in_dim(inputs, (here ^ m) * slab, slab, 1) for m in chosen], axis=1
        )
        product = lax.dot_general(
            picked, grad_value, (((0,), (0,)), ((), ())), preferred_element_type=f32
        )
        sides.append((product * wscale).astype(jnp.bfloat16))
    arrived = exchange(sides[0], "seq", first_bit)
    paired = sides[1].astype(f32) + arrived.astype(f32)
    half = width // 2
    outs = []
    for at, order in ((0, rest), (half, rest[::-1])):
        terms = {
            m: paired[k * slab : (k + 1) * slab, at : at + half].astype(jnp.bfloat16)
            for k, m in enumerate(chosen)
        }
        outs.append(halving(terms, "seq", order))
    grad_weight = jnp.concatenate(outs, axis=1).astype(f32)
    return (grad_input, grad_query, grad_key, grad_value, grad_weight)


def solution(mesh):
    in_specs = (
        P("seq", None),
        P("seq", "head"),
        P("seq", "head"),
        P("seq", "head"),
        P("seq", "head"),
        P("seq", "head"),
    )
    out_specs = (
        P("seq", "head"),
        P("seq", "head"),
        P("seq", "head"),
        P("seq", "head"),
        P("seq", "head"),
    )
    return jax.shard_map(local, mesh=mesh, in_specs=in_specs, out_specs=out_specs, check_vma=False)
```

```python
import math

import jax
import jax.numpy as jnp
from jax import lax
from jax.sharding import PartitionSpec as P


HEAD_DIM = 128


def exchange(x, axis, bit):
    return lax.ppermute(x, axis, [(i, i ^ bit) for i in range(lax.axis_size(axis))])


def bits_of(axis):
    count = lax.axis_size(axis)
    assert count & (count - 1) == 0
    return [1 << k for k in range(count.bit_length() - 1)]


def carried_in(state, axis, later):
    here = lax.axis_index(axis)
    carried, total = jnp.zeros_like(state), state
    for bit in bits_of(axis):
        got = exchange(total.astype(jnp.bfloat16), axis, bit).astype(state.dtype)
        upper = (here & bit) != 0
        carried = carried + jnp.where(upper != later, got, 0.0)
        total = total + got
    return carried


def halving(terms, axis, bits):
    terms = dict(terms)
    for at, bit in enumerate(bits):
        leaving = [m for m in terms if m & bit]
        ahead = sum(bits[at + 1 :])
        for m in sorted(leaving, key=lambda m: -bin(m & ahead).count("1")):
            got = exchange(terms.pop(m).astype(jnp.bfloat16), axis, bit)
            terms[m ^ bit] = terms[m ^ bit].astype(jnp.float32) + got.astype(jnp.float32)
    return terms[0]


def spread(block, axis):
    first_bit, *rest = bits_of(axis)
    half = block.shape[0] // 2
    found = {0: (block[:half], block[half:])}
    whole = {0: block}
    for m in sorted(range(2, lax.axis_size(axis), 2), key=lambda m: (bin(m).count("1"), m)):
        low, high = m & -m, 1 << (m.bit_length() - 1)
        if low == high:
            whole[m] = exchange(block, axis, m)
            found[m] = (whole[m][:half], whole[m][half:])
        else:
            found[m] = (
                exchange(found[m ^ low][0], axis, low),
                exchange(found[m ^ high][1], axis, high),
            )
    for m in list(found):
        if m in whole:
            got = exchange(whole[m], axis, first_bit)
            found[m | first_bit] = (got[:half], got[half:])
        else:
            found[m | first_bit] = tuple(exchange(x, axis, first_bit) for x in found[m])
    return found


def local(inputs, queries, keys, values, out_grad, value_weight):
    f32 = jnp.float32
    high = lax.Precision.HIGHEST
    rows = queries.shape[0]
    width = queries.shape[1]
    nheads = width // HEAD_DIM
    first = lax.axis_index("seq") * rows
    posit = (first + jnp.arange(rows, dtype=jnp.int32)).astype(f32)
    factor = 1.0 / jnp.sqrt(HEAD_DIM * (posit + 1.0))
    q3 = queries.reshape(rows, nheads, HEAD_DIM)
    k3 = keys.reshape(rows, nheads, HEAD_DIM)
    v3 = values.reshape(rows, nheads, HEAD_DIM)
    o3 = out_grad.reshape(rows, nheads, HEAD_DIM)
    o3wide = o3.astype(f32)
    state_kv = jnp.einsum("thi,thj->hij", k3, v3, preferred_element_type=f32)
    state_qo = jnp.einsum(
        "thi,thj->hij", q3.astype(f32), o3wide * factor[:, None, None], precision=high
    )
    suffix = carried_in(state_qo, "seq", True)
    prefix = carried_in(state_kv, "seq", False)
    index = jnp.arange(rows, dtype=jnp.int32)
    lower = (index[:, None] >= index[None, :])[None]
    score_qk = (
        jnp.einsum("thd,shd->hts", q3, k3, preferred_element_type=f32) * factor[None, :, None]
    )
    score_qk = jnp.where(lower, score_qk, 0.0).astype(jnp.bfloat16)
    score_ov = (
        jnp.einsum("thd,shd->hts", o3, v3, preferred_element_type=f32) * factor[None, :, None]
    )
    score_ov = jnp.where(lower, score_ov, 0.0).astype(jnp.bfloat16)
    dq = jnp.einsum("hts,shd->thd", score_ov, k3, preferred_element_type=f32)
    dq = dq + factor[:, None, None] * jnp.einsum("thj,hij->thi", o3wide, prefix, precision=high)
    dk = jnp.einsum("hts,thd->shd", score_ov, q3, preferred_element_type=f32)
    dk = dk + jnp.einsum("shj,hij->shi", v3.astype(f32), suffix, precision=high)
    dv = jnp.einsum("hts,thd->shd", score_qk, o3, preferred_element_type=f32)
    dv = dv + jnp.einsum("shi,hij->shj", k3.astype(f32), suffix, precision=high)
    grad_query = dq.reshape(rows, width).astype(jnp.bfloat16)
    grad_key = dk.reshape(rows, width).astype(jnp.bfloat16)
    grad_value = dv.reshape(rows, width).astype(jnp.bfloat16)
    here, group = (lax.axis_index("seq"), lax.axis_index("head"))
    seqs, heads = (lax.axis_size("seq"), lax.axis_size("head"))
    found = spread(value_weight, "seq")
    weight = jnp.concatenate([x for m in range(seqs) for x in found[m]], axis=0)
    span = value_weight.shape[0]
    each = seqs // heads
    pieces = {}
    for m in range(heads):
        for j in range(each):
            at = here ^ ((group ^ m) * each + j)
            part = lax.dynamic_slice_in_dim(weight, at * span, span, 0)
            pieces[m, j] = lax.dot_general(
                grad_value, part, (((1,), (1,)), ((), ())), preferred_element_type=f32
            ).astype(jnp.bfloat16)
    leaving = [key for key in pieces if key[0] & 1]
    late_value, *ready = lax.optimization_barrier((grad_value, *[pieces[key] for key in leaving]))
    pieces.update(zip(leaving, ready))
    grad_input = jnp.concatenate(
        [
            halving({m: pieces[m, j] for m in range(heads)}, "head", bits_of("head"))
            for j in range(each)
        ],
        axis=1,
    ).astype(jnp.bfloat16)
    wscale = 1.0 / math.sqrt(rows * lax.axis_size("seq"))
    slab = inputs.shape[1] // seqs
    first_bit, *rest = bits_of("seq")
    sides = []
    for side in (first_bit, 0):
        chosen = [m for m in range(seqs) if m & first_bit == side]
        picked = jnp.concatenate(
            [lax.dynamic_slice_in_dim(inputs, (here ^ m) * slab, slab, 1) for m in chosen], axis=1
        )
        product = lax.dot_general(
            picked, late_value, (((0,), (0,)), ((), ())), preferred_element_type=f32
        )
        sides.append((product * wscale).astype(jnp.bfloat16))
    arrived = exchange(sides[0], "seq", first_bit)
    paired = sides[1].astype(f32) + arrived.astype(f32)
    half = width // 2
    outs = []
    for at, order in ((0, rest), (half, rest[::-1])):
        terms = {
            m: paired[k * slab : (k + 1) * slab, at : at + half].astype(jnp.bfloat16)
            for k, m in enumerate(chosen)
        }
        terms = {m: lax.optimization_barrier(x) if m else x for m, x in terms.items()}
        outs.append(halving(terms, "seq", order))
    grad_weight = jnp.concatenate(outs, axis=1).astype(f32)
    return (grad_input, grad_query, grad_key, grad_value, grad_weight)


def solution(mesh):
    in_specs = (
        P("seq", None),
        P("seq", "head"),
        P("seq", "head"),
        P("seq", "head"),
        P("seq", "head"),
        P("seq", "head"),
    )
    out_specs = (
        P("seq", "head"),
        P("seq", "head"),
        P("seq", "head"),
        P("seq", "head"),
        P("seq", "head"),
    )

    return jax.shard_map(local, mesh=mesh, in_specs=in_specs, out_specs=out_specs, check_vma=False)
```

```python
import math

import jax
import jax.numpy as jnp
from jax import lax
from jax.sharding import PartitionSpec as P


HEAD_DIM = 128


def exchange(x, axis, bit):
    return lax.ppermute(x, axis, [(i, i ^ bit) for i in range(lax.axis_size(axis))])


def bits_of(axis):
    count = lax.axis_size(axis)
    assert count & (count - 1) == 0
    return [1 << k for k in range(count.bit_length() - 1)]


def carried_in(forward, backward, axis):
    here = lax.axis_index(axis)
    total = jnp.stack([forward, backward])
    carried = jnp.zeros_like(total)
    for bit in bits_of(axis):
        got = exchange(total.astype(jnp.bfloat16), axis, bit).astype(total.dtype)
        upper = (here & bit) != 0
        wanted = jnp.stack([upper, ~upper])[:, None, None, None]
        carried = carried + jnp.where(wanted, got, 0.0)
        total = total + got
    return carried[0], carried[1]


def halving(terms, axis, bits):
    terms = dict(terms)
    for at, bit in enumerate(bits):
        leaving = [m for m in terms if m & bit]
        ahead = sum(bits[at + 1 :])
        for m in sorted(leaving, key=lambda m: -bin(m & ahead).count("1")):
            got = exchange(terms.pop(m).astype(jnp.bfloat16), axis, bit)
            terms[m ^ bit] = terms[m ^ bit].astype(jnp.float32) + got.astype(jnp.float32)
    return terms[0]


def spread(block, axis):
    first_bit, *rest = bits_of(axis)
    half = block.shape[0] // 2
    found = {0: (block[:half], block[half:])}
    whole = {0: block}
    for m in sorted(range(2, lax.axis_size(axis), 2), key=lambda m: (bin(m).count("1"), m)):
        low, high = m & -m, 1 << (m.bit_length() - 1)
        if low == high:
            whole[m] = exchange(block, axis, m)
            found[m] = (whole[m][:half], whole[m][half:])
        else:
            found[m] = (
                exchange(found[m ^ low][0], axis, low),
                exchange(found[m ^ high][1], axis, high),
            )
    for m in list(found):
        if m in whole:
            got = exchange(whole[m], axis, first_bit)
            found[m | first_bit] = (got[:half], got[half:])
        else:
            found[m | first_bit] = tuple(exchange(x, axis, first_bit) for x in found[m])
    return found


def local(inputs, queries, keys, values, out_grad, value_weight):
    f32 = jnp.float32
    high = lax.Precision.HIGHEST
    rows = queries.shape[0]
    width = queries.shape[1]
    nheads = width // HEAD_DIM
    first = lax.axis_index("seq") * rows
    posit = (first + jnp.arange(rows, dtype=jnp.int32)).astype(f32)
    factor = 1.0 / jnp.sqrt(HEAD_DIM * (posit + 1.0))
    q3 = queries.reshape(rows, nheads, HEAD_DIM)
    k3 = keys.reshape(rows, nheads, HEAD_DIM)
    v3 = values.reshape(rows, nheads, HEAD_DIM)
    o3 = out_grad.reshape(rows, nheads, HEAD_DIM)
    o3wide = o3.astype(f32)
    state_kv = jnp.einsum("thi,thj->hij", k3, v3, preferred_element_type=f32)
    state_qo = jnp.einsum(
        "thi,thj->hij", q3.astype(f32), o3wide * factor[:, None, None], precision=high
    )
    prefix, suffix = carried_in(state_kv, state_qo, "seq")
    index = jnp.arange(rows, dtype=jnp.int32)
    lower = (index[:, None] >= index[None, :])[None]
    score_qk = (
        jnp.einsum("thd,shd->hts", q3, k3, preferred_element_type=f32) * factor[None, :, None]
    )
    score_qk = jnp.where(lower, score_qk, 0.0).astype(jnp.bfloat16)
    score_ov = (
        jnp.einsum("thd,shd->hts", o3, v3, preferred_element_type=f32) * factor[None, :, None]
    )
    score_ov = jnp.where(lower, score_ov, 0.0).astype(jnp.bfloat16)
    dq = jnp.einsum("hts,shd->thd", score_ov, k3, preferred_element_type=f32)
    dq = dq + factor[:, None, None] * jnp.einsum("thj,hij->thi", o3wide, prefix, precision=high)
    dk = jnp.einsum("hts,thd->shd", score_ov, q3, preferred_element_type=f32)
    dk = dk + jnp.einsum("shj,hij->shi", v3.astype(f32), suffix, precision=high)
    dv = jnp.einsum("hts,thd->shd", score_qk, o3, preferred_element_type=f32)
    dv = dv + jnp.einsum("shi,hij->shj", k3.astype(f32), suffix, precision=high)
    grad_query = dq.reshape(rows, width).astype(jnp.bfloat16)
    grad_key = dk.reshape(rows, width).astype(jnp.bfloat16)
    grad_value = dv.reshape(rows, width).astype(jnp.bfloat16)
    here, group = (lax.axis_index("seq"), lax.axis_index("head"))
    seqs, heads = (lax.axis_size("seq"), lax.axis_size("head"))
    found = spread(value_weight, "seq")
    weight = jnp.concatenate([x for m in range(seqs) for x in found[m]], axis=0)
    span = value_weight.shape[0]
    each = seqs // heads
    pieces = {}
    for m in range(heads):
        for j in range(each):
            at = here ^ ((group ^ m) * each + j)
            part = lax.dynamic_slice_in_dim(weight, at * span, span, 0)
            pieces[m, j] = lax.dot_general(
                grad_value, part, (((1,), (1,)), ((), ())), preferred_element_type=f32
            ).astype(jnp.bfloat16)
    leaving = [key for key in pieces if key[0] & 1]
    late_value, *ready = lax.optimization_barrier((grad_value, *[pieces[key] for key in leaving]))
    pieces.update(zip(leaving, ready))
    grad_input = jnp.concatenate(
        [
            halving({m: pieces[m, j] for m in range(heads)}, "head", bits_of("head"))
            for j in range(each)
        ],
        axis=1,
    ).astype(jnp.bfloat16)
    wscale = 1.0 / math.sqrt(rows * lax.axis_size("seq"))
    slab = inputs.shape[1] // seqs
    first_bit, *rest = bits_of("seq")
    sides = []
    for side in (first_bit, 0):
        chosen = [m for m in range(seqs) if m & first_bit == side]
        picked = jnp.concatenate(
            [lax.dynamic_slice_in_dim(inputs, (here ^ m) * slab, slab, 1) for m in chosen], axis=1
        )
        product = lax.dot_general(
            picked, late_value, (((0,), (0,)), ((), ())), preferred_element_type=f32
        )
        sides.append((product * wscale).astype(jnp.bfloat16))
    arrived = exchange(sides[0], "seq", first_bit)
    paired = sides[1].astype(f32) + arrived.astype(f32)
    half = width // 2
    outs = []
    for at, order in ((0, rest), (half, rest[::-1])):
        terms = {
            m: paired[k * slab : (k + 1) * slab, at : at + half].astype(jnp.bfloat16)
            for k, m in enumerate(chosen)
        }
        terms = {m: lax.optimization_barrier(x) if m else x for m, x in terms.items()}
        outs.append(halving(terms, "seq", order))
    grad_weight = jnp.concatenate(outs, axis=1).astype(f32)
    return (grad_input, grad_query, grad_key, grad_value, grad_weight)


def solution(mesh):
    in_specs = (
        P("seq", None),
        P("seq", "head"),
        P("seq", "head"),
        P("seq", "head"),
        P("seq", "head"),
        P("seq", "head"),
    )
    out_specs = (
        P("seq", "head"),
        P("seq", "head"),
        P("seq", "head"),
        P("seq", "head"),
        P("seq", "head"),
    )

    return jax.shard_map(local, mesh=mesh, in_specs=in_specs, out_specs=out_specs, check_vma=False)
```
